512 devices in a mesh: occ: 16 (over y, z_hi), vir: 32 (over x, z_lo, core).
Axes of the slice: x: 4, y: 4, z: 16 (z_hi: 4, z_lo: 4; z = z_hi * 4 + z_lo), core: 2. Of those that a mesh axis runs over, the one named last changes fastest.
Arguments:
- amplitudes: float32 [4, 1024, 1024], P(None, 'occ', 'vir'), may hold values from -6 to 6
- integrals: float32 [4, 28672, 1024], P(None, 'vir', 'occ'), may hold values from -0.1875 to 0.1875
Outputs:
- ladder: float32 [4, 1024, 28672], P(None, 'occ', 'vir')
The draws below stay inside these ranges and needn't reach their ends.
All inputs are finite; a program needn't handle non-finite values.
Results may differ from the reference program's by a relative error of at most 0.000073.
Values sent between devices are 32-bit elements; how exact they have to be, the bound alone decides.
A program may use at most 64 MiB of HBM per device.

```python
import jax
import jax.numpy as jnp
from jax import lax

NIRREP = 4
IJ_G = 1024
CD_G = 1024
AB_G = 28672


def shard_levels(key, dims, cuts, low, largest):
    def one(dim, shards_of):
        steps = jax.random.uniform(jax.random.fold_in(jax.random.fold_in(key, 6), dim), (shards_of,), jnp.float32, low / len(cuts), largest / len(cuts))
        return jnp.repeat(jnp.exp(steps), dims[dim] // shards_of).reshape((-1,) + (1,) * (len(dims) - dim - 1))

    gain = one(*cuts[0])
    for cut in cuts[1:]:
        gain = gain * one(*cut)
    return gain


def bell_draw(stream_key, shape, width, bound, split=(), kind=jnp.bfloat16):
    result = jax.random.normal(stream_key, shape, jnp.float32) * width
    if len(split) > 0:
        result = shard_levels(stream_key, shape, split, -0.22, 0.18) * result
    return jnp.clip(result, min=-bound, max=bound).astype(kind)


def setup_inputs(seed: int = 0) -> dict:
    streams_of = jax.random.split(jax.random.key(seed), 3)
    amplitudes = bell_draw(streams_of[0], (NIRREP, IJ_G, CD_G), 1.0, 6.0, ((1, 16), (2, 32)), jnp.float32)
    integrals = bell_draw(streams_of[1], (NIRREP, AB_G, CD_G), CD_G ** -0.5, 0.1875, ((1, 32), (2, 16)), jnp.float32)
    return {"amplitudes": amplitudes, "integrals": integrals}


def reference(amplitudes, integrals):
    panel_sum = lax.dot_general(amplitudes, integrals, (((2,), (2,)), ((0,), (0,))), precision=lax.Precision.HIGHEST, preferred_element_type=jnp.float32)
    return 0.5 * panel_sum
```

```python
import jax
import jax.numpy as jnp
from jax import lax
from jax.experimental import pallas as pl
from jax.experimental.pallas import tpu as pltpu
from jax.sharding import PartitionSpec as P

MESH = pl.DeviceIdType.MESH
CHUNK = 128
AHEAD = 3
LAG = 4


def kernel(
    at_ref, bt_ref, out_ref, pk, ag, at, a_hi, a_lo, bt, cb,
    a_send, a_recv, b_send, b_recv, up_send, up_recv, dn_send, dn_recv, ru_send, rd_send, far_recv, c_send, c_recv,
):
    o, v = lax.axis_index("occ"), lax.axis_index("vir")
    y, zh = o // 4, o % 4
    x, zl, c = v // 8, (v // 2) % 4, v % 2
    z = zh * 4 + zl
    zc = (z + 14) % 16
    g, zs = zc // 4, zc % 4
    chunks = bt.shape[0]
    y_up, y_dn = (y + 1) % 4, (y + 3) % 4

    def device(z_, y_=y, x_=x, c_=c):
        w = z_ % 16
        return (y_ * 4 + w // 4, (x_ * 4 + w % 4) * 2 + c_)

    def remote(src, dst, send, recv, where):
        return pltpu.make_async_remote_copy(
            src_ref=src, dst_ref=dst, send_sem=send, recv_sem=recv, device_id=where, device_id_type=MESH
        )

    def drain(ref, sem):
        pltpu.make_async_copy(ref, ref, sem).wait()

    pk[:, :, 0:64] = at_ref[:, 0:16, :]
    pk[:, :, 64:128] = at_ref[:, 16:32, :]

    barrier = pltpu.get_barrier_semaphore()
    greet = [device(z + d) for d in (2, 6, 10, 14)]
    greet += [device(4 * g + 2 + (zs + d) % 4) for d in (1, 2, 3)]
    greet += [device(z, y_=y_up), device(z, y_=y_dn)]
    greet += [device(z, x_=(x + d) % 4) for d in (1, 2, 3)]
    greet += [device(z, c_=1 - c)]
    for where in greet:
        pl.semaphore_signal(barrier, inc=1, device_id=where, device_id_type=MESH)
    pl.semaphore_wait(barrier, len(greet))

    def lanes(s):
        return pl.ds(pl.multiple_of(s * CHUNK, CHUNK), CHUNK)

    def rows(start, size):
        return pl.ds(pl.multiple_of(start, 64), size)

    def send_b(s):
        for h in range(4):
            remote(
                bt_ref.at[h, :, lanes(s)], bt.at[s, rows(o * 64, 64)], b_send, b_recv.at[s], device(zl + 4 * h + 2)
            ).start()

    for h in range(4):
        remote(pk.at[h], ag.at[c, x, zl, zh], a_send.at[0], a_recv.at[0], device(zl + 4 * h + 2)).start()
    for s in range(AHEAD):
        send_b(s)

    own = rows(y * 256, 256)
    from_dn = rows(y_dn * 256, 256)
    from_up = rows(y_up * 256, 256)
    far = rows(((y + 2) % 4) * 256, 256)
    up_half = rows(y_dn * 256, 128)
    dn_half = rows(y_up * 256 + 128, 128)

    def step(s, carry):
        @pl.when(s < chunks)
        def _():
            drain(bt.at[s, own], b_recv.at[s])
            remote(bt.at[s, own], bt.at[s, own], up_send, up_recv.at[s], device(z, y_=y_up)).start()
            remote(bt.at[s, own], bt.at[s, own], dn_send, dn_recv.at[s], device(z, y_=y_dn)).start()

        @pl.when(s == 0)
        def _():
            drain(ag.at[c, x, zs], a_recv.at[0])
            for d in (1, 2, 3):
                there = device(4 * g + 2 + (zs + d) % 4)
                remote(ag.at[c, x, zs], ag.at[c, x, zs], a_send.at[1], a_recv.at[1], there).start()

        @pl.when(s + AHEAD < chunks)
        def _():
            send_b(s + AHEAD)

        @pl.when(jnp.logical_and(s >= 1, s < chunks + 1))
        def _():
            t = s - 1
            drain(bt.at[t, from_dn], up_recv.at[t])
            remote(bt.at[t, up_half], bt.at[t, up_half], ru_send, far_recv.at[t], device(z, y_=y_up)).start()
            drain(bt.at[t, from_up], dn_recv.at[t])
            remote(bt.at[t, dn_half], bt.at[t, dn_half], rd_send, far_recv.at[t], device(z, y_=y_dn)).start()

        @pl.when(s == 2)
        def _():
            drain(ag.at[c, x, pl.ds(0, 3)], a_recv.at[1])
            for d in (1, 2, 3):
                there = device(z, x_=(x + d) % 4)
                remote(ag.at[c, x], ag.at[c, x], a_send.at[2], a_recv.at[2], there).start()

        @pl.when(s == 3)
        def _():
            drain(ag.at[c, pl.ds(0, 3)], a_recv.at[2])
            remote(ag.at[c], ag.at[c], a_send.at[3], a_recv.at[3], device(z, c_=1 - c)).start()

        @pl.when(s == LAG)
        def _():
            drain(ag.at[1 - c], a_recv.at[3])

            def unpack(u, carry):
                low = lax.broadcasted_iota(jnp.int32, (16, 128), 1) < 64
                part = [ag[u % 2, u // 8, (u // 2) % 4, h] for h in range(4)]
                turned = [pltpu.roll(p, 64, 1) for p in part]
                for h in (0, 2):
                    side = pl.ds(64 * h, 128)
                    at[pl.ds(pl.multiple_of(u * 32, 16), 16), side] = jnp.where(low, part[h], turned[h + 1])
                    at[pl.ds(pl.multiple_of(u * 32 + 16, 16), 16), side] = jnp.where(low, turned[h], part[h + 1])
                return carry

            lax.fori_loop(0, 32, unpack, 0)

            def turn(k, carry):
                block = at[pl.ds(pl.multiple_of(k * 128, 128), 128), :].T
                high = block.astype(jnp.bfloat16)
                a_hi[:, pl.ds(pl.multiple_of(k * 128, 128), 128)] = high
                a_lo[:, pl.ds(pl.multiple_of(k * 128, 128), 128)] = (block - high.astype(jnp.float32)).astype(jnp.bfloat16)
                return carry

            lax.fori_loop(0, 8, turn, 0)

        @pl.when(s >= LAG)
        def _():
            t = s - LAG
            drain(bt.at[t, far], far_recv.at[t])
            block = bt[t]
            high = block.astype(jnp.bfloat16)
            low = (block - high.astype(jnp.float32)).astype(jnp.bfloat16)
            both = jnp.dot(a_hi[...], jnp.concatenate([high, low], axis=1), preferred_element_type=jnp.float32)
            cross = jnp.dot(a_lo[...], high, preferred_element_type=jnp.float32)
            cb[t] = 0.5 * (both[:, 0:CHUNK] + (both[:, CHUNK:] + cross))
            for h in range(4):
                remote(
                    cb.at[t, pl.ds(64 * h, 64)], out_ref.at[g, :, lanes(t)], c_send, c_recv, device(4 * h + zs)
                ).start()

        return carry

    lax.fori_loop(0, chunks + LAG, step, 0)

    drain(out_ref, c_recv)
    drain(pk, a_send.at[0])
    drain(ag.at[c, x, pl.ds(0, 3)], a_send.at[1])
    drain(ag.at[c, pl.ds(0, 3)], a_send.at[2])
    drain(ag.at[c], a_send.at[3])
    drain(bt_ref, b_send)
    drain(cb, up_send)
    drain(cb, dn_send)
    drain(cb.at[:, pl.ds(0, 128)], ru_send)
    drain(cb.at[:, pl.ds(0, 128)], rd_send)
    drain(cb, c_send)


def body(amplitudes, integrals):
    at = jnp.swapaxes(amplitudes, 1, 2)
    bt = jnp.swapaxes(integrals, 1, 2)
    n_g, depth, cols = bt.shape
    chunks = cols // CHUNK
    f32, bf16 = jnp.float32, jnp.bfloat16
    dma = pltpu.SemaphoreType.DMA
    return pl.pallas_call(
        kernel,
        out_shape=jax.ShapeDtypeStruct((n_g, 64, cols), f32),
        in_specs=[pl.BlockSpec(memory_space=pltpu.VMEM), pl.BlockSpec(memory_space=pl.ANY)],
        out_specs=pl.BlockSpec(memory_space=pl.ANY),
        scratch_shapes=[
            pltpu.VMEM((4, 16, 128), f32),
            pltpu.VMEM((2, 4, 4, 4, 16, 128), f32),
            pltpu.VMEM((1024, 256), f32),
            pltpu.VMEM((256, 1024), bf16),
            pltpu.VMEM((256, 1024), bf16),
            pltpu.VMEM((chunks, 1024, CHUNK), f32),
            pltpu.VMEM((chunks, 256, CHUNK), f32),
            dma((4,)),
            dma((4,)),
            dma,
            dma((chunks,)),
            dma,
            dma((chunks,)),
            dma,
            dma((chunks,)),
            dma,
            dma,
            dma((chunks,)),
            dma,
            dma,
        ],
        compiler_params=pltpu.CompilerParams(collective_id=0, has_side_effects=True),
    )(at, bt)


def solution(mesh):
    in_specs = (P(None, "occ", "vir"), P(None, "vir", "occ"))
    out_specs = P(None, "occ", "vir")
    return jax.shard_map(body, mesh=mesh, in_specs=in_specs, out_specs=out_specs, check_vma=False)
```

```python
import jax
import jax.numpy as jnp
from jax import lax
from jax.experimental import pallas as pl
from jax.experimental.pallas import tpu as pltpu
from jax.sharding import PartitionSpec as P

MESH = pl.DeviceIdType.MESH
CHUNK = 128
AHEAD = 3
LAG = 4
ORDER = (1, 2, 0, 3)


def kernel(
    at_ref, bt_ref, out_ref, pk, ag, at, a_hi, a_lo, bt, cb,
    a_send, a_recv, b_send, b_recv, up_send, up_recv, dn_send, dn_recv, ru_send, rd_send, far_recv, c_send, c_recv,
):
    o, v = lax.axis_index("occ"), lax.axis_index("vir")
    y, zh = o // 4, o % 4
    x, zl, c = v // 8, (v // 2) % 4, v % 2
    z = zh * 4 + zl
    zc = (z + 14) % 16
    g, zs = zc // 4, zc % 4
    chunks = bt.shape[0]
    y_up, y_dn = (y + 1) % 4, (y + 3) % 4

    def device(z_, y_=y, x_=x, c_=c):
        w = z_ % 16
        return (y_ * 4 + w // 4, (x_ * 4 + w % 4) * 2 + c_)

    def remote(src, dst, send, recv, where):
        return pltpu.make_async_remote_copy(
            src_ref=src, dst_ref=dst, send_sem=send, recv_sem=recv, device_id=where, device_id_type=MESH
        )

    def drain(ref, sem):
        pltpu.make_async_copy(ref, ref, sem).wait()

    pk[:, :, 0:64] = at_ref[:, 0:16, :]
    pk[:, :, 64:128] = at_ref[:, 16:32, :]

    barrier = pltpu.get_barrier_semaphore()
    greet = [device(z + d) for d in (2, 6, 10, 14)]
    greet += [device(4 * g + 2 + (zs + d) % 4) for d in (1, 2, 3)]
    greet += [device(z, y_=y_up), device(z, y_=y_dn)]
    greet += [device(z, x_=(x + d) % 4) for d in (1, 2, 3)]
    greet += [device(z, c_=1 - c)]
    for where in greet:
        pl.semaphore_signal(barrier, inc=1, device_id=where, device_id_type=MESH)
    pl.semaphore_wait(barrier, len(greet))

    def lanes(s):
        return pl.ds(pl.multiple_of(s * CHUNK, CHUNK), CHUNK)

    def rows(start, size):
        return pl.ds(pl.multiple_of(start, 64), size)

    def send_b(s):
        for i in ORDER:
            h = (zh + i) % 4
            remote(
                bt_ref.at[h, :, lanes(s)], bt.at[s, rows(o * 64, 64)], b_send, b_recv.at[s], device(zl + 4 * h + 2)
            ).start()

    for i in ORDER:
        h = (zh + i) % 4
        remote(pk.at[h], ag.at[c, x, zl, zh], a_send.at[0], a_recv.at[0], device(zl + 4 * h + 2)).start()
    for s in range(AHEAD):
        send_b(s)

    own = rows(y * 256, 256)
    from_dn = rows(y_dn * 256, 256)
    from_up = rows(y_up * 256, 256)
    far = rows(((y + 2) % 4) * 256, 256)
    up_half = rows(y_dn * 256, 128)
    dn_half = rows(y_up * 256 + 128, 128)

    def step(s, carry):
        @pl.when(s < chunks)
        def _():
            drain(bt.at[s, own], b_recv.at[s])
            remote(bt.at[s, own], bt.at[s, own], up_send, up_recv.at[s], device(z, y_=y_up)).start()
            remote(bt.at[s, own], bt.at[s, own], dn_send, dn_recv.at[s], device(z, y_=y_dn)).start()

        @pl.when(s == 0)
        def _():
            drain(ag.at[c, x, zs], a_recv.at[0])
            for d in (1, 2, 3):
                there = device(4 * g + 2 + (zs + d) % 4)
                remote(ag.at[c, x, zs], ag.at[c, x, zs], a_send.at[1], a_recv.at[1], there).start()

        @pl.when(s + AHEAD < chunks)
        def _():
            send_b(s + AHEAD)

        @pl.when(jnp.logical_and(s >= 1, s < chunks + 1))
        def _():
            t = s - 1
            drain(bt.at[t, from_dn], up_recv.at[t])
            remote(bt.at[t, up_half], bt.at[t, up_half], ru_send, far_recv.at[t], device(z, y_=y_up)).start()
            drain(bt.at[t, from_up], dn_recv.at[t])
            remote(bt.at[t, dn_half], bt.at[t, dn_half], rd_send, far_recv.at[t], device(z, y_=y_dn)).start()

        @pl.when(s == 2)
        def _():
            drain(ag.at[c, x, pl.ds(0, 3)], a_recv.at[1])
            for d in (1, 2, 3):
                there = device(z, x_=(x + d) % 4)
                remote(ag.at[c, x], ag.at[c, x], a_send.at[2], a_recv.at[2], there).start()

        @pl.when(s == 3)
        def _():
            drain(ag.at[c, pl.ds(0, 3)], a_recv.at[2])
            remote(ag.at[c], ag.at[c], a_send.at[3], a_recv.at[3], device(z, c_=1 - c)).start()

        @pl.when(s == LAG)
        def _():
            drain(ag.at[1 - c], a_recv.at[3])

            def unpack(u, carry):
                low = lax.broadcasted_iota(jnp.int32, (16, 128), 1) < 64
                part = [ag[u % 2, u // 8, (u // 2) % 4, h] for h in range(4)]
                turned = [pltpu.roll(p, 64, 1) for p in part]
                for h in (0, 2):
                    side = pl.ds(64 * h, 128)
                    at[pl.ds(pl.multiple_of(u * 32, 16), 16), side] = jnp.where(low, part[h], turned[h + 1])
                    at[pl.ds(pl.multiple_of(u * 32 + 16, 16), 16), side] = jnp.where(low, turned[h], part[h + 1])
                return carry

            lax.fori_loop(0, 32, unpack, 0)

            def turn(k, carry):
                block = at[pl.ds(pl.multiple_of(k * 128, 128), 128), :].T
                high = block.astype(jnp.bfloat16)
                a_hi[:, pl.ds(pl.multiple_of(k * 128, 128), 128)] = high
                a_lo[:, pl.ds(pl.multiple_of(k * 128, 128), 128)] = (block - high.astype(jnp.float32)).astype(jnp.bfloat16)
                return carry

            lax.fori_loop(0, 8, turn, 0)

        @pl.when(s >= LAG)
        def _():
            t = s - LAG
            drain(bt.at[t, far], far_recv.at[t])
            block = bt[t]
            high = block.astype(jnp.bfloat16)
            low = (block - high.astype(jnp.float32)).astype(jnp.bfloat16)
            both = jnp.dot(a_hi[...], jnp.concatenate([high, low], axis=1), preferred_element_type=jnp.float32)
            cross = jnp.dot(a_lo[...], high, preferred_element_type=jnp.float32)
            cb[t] = 0.5 * (both[:, 0:CHUNK] + (both[:, CHUNK:] + cross))
            for i in ORDER:
                h = ((z + 2 + 4 * i) % 16) // 4
                remote(
                    cb.at[t, rows(64 * h, 64)], out_ref.at[g, :, lanes(t)], c_send, c_recv, device(4 * h + zs)
                ).start()

        return carry

    lax.fori_loop(0, chunks + LAG, step, 0)

    drain(out_ref, c_recv)
    drain(pk, a_send.at[0])
    drain(ag.at[c, x, pl.ds(0, 3)], a_send.at[1])
    drain(ag.at[c, pl.ds(0, 3)], a_send.at[2])
    drain(ag.at[c], a_send.at[3])
    drain(bt_ref, b_send)
    drain(cb, up_send)
    drain(cb, dn_send)
    drain(cb.at[:, pl.ds(0, 128)], ru_send)
    drain(cb.at[:, pl.ds(0, 128)], rd_send)
    drain(cb, c_send)


def body(amplitudes, integrals):
    at = jnp.swapaxes(amplitudes, 1, 2)
    bt = pltpu.with_memory_space_constraint(jnp.swapaxes(integrals, 1, 2), pltpu.HBM)
    n_g, depth, cols = bt.shape
    chunks = cols // CHUNK
    f32, bf16 = jnp.float32, jnp.bfloat16
    dma = pltpu.SemaphoreType.DMA
    return pl.pallas_call(
        kernel,
        out_shape=jax.ShapeDtypeStruct((n_g, 64, cols), f32),
        in_specs=[pl.BlockSpec(memory_space=pltpu.VMEM), pl.BlockSpec(memory_space=pl.ANY)],
        out_specs=pl.BlockSpec(memory_space=pl.ANY),
        scratch_shapes=[
            pltpu.VMEM((4, 16, 128), f32),
            pltpu.VMEM((2, 4, 4, 4, 16, 128), f32),
            pltpu.VMEM((1024, 256), f32),
            pltpu.VMEM((256, 1024), bf16),
            pltpu.VMEM((256, 1024), bf16),
            pltpu.VMEM((chunks, 1024, CHUNK), f32),
            pltpu.VMEM((chunks, 256, CHUNK), f32),
            dma((4,)),
            dma((4,)),
            dma,
            dma((chunks,)),
            dma,
            dma((chunks,)),
            dma,
            dma((chunks,)),
            dma,
            dma,
            dma((chunks,)),
            dma,
            dma,
        ],
        compiler_params=pltpu.CompilerParams(collective_id=0, has_side_effects=True, vmem_limit_bytes=20 * 2**20),
    )(at, bt)


def solution(mesh):
    in_specs = (P(None, "occ", "vir"), P(None, "vir", "occ"))
    out_specs = P(None, "occ", "vir")
    return jax.shard_map(body, mesh=mesh, in_specs=in_specs, out_specs=out_specs, check_vma=False)
```

```python
import jax
import jax.numpy as jnp
from jax import lax
from jax.experimental import pallas as pl
from jax.experimental.pallas import tpu as pltpu
from jax.sharding import PartitionSpec as P

MESH = pl.DeviceIdType.MESH
CHUNK = 128
AHEAD = 3
LAG = 4
ORDER = (1, 2, 0, 3)


def kernel(
    at_ref, bt_ref, out_ref, an, pk, ag, at, a_hi, a_lo, bt, cb,
    a_send, a_recv, b_send, b_recv, up_send, up_recv, dn_send, dn_recv, ru_send, rd_send, far_recv, c_send, c_recv, fetched,
):
    o, v = lax.axis_index("occ"), lax.axis_index("vir")
    y, zh = o // 4, o % 4
    x, zl, c = v // 8, (v // 2) % 4, v % 2
    z = zh * 4 + zl
    zc = (z + 14) % 16
    g, zs = zc // 4, zc % 4
    chunks = bt.shape[0]
    y_up, y_dn = (y + 1) % 4, (y + 3) % 4

    def device(z_, y_=y, x_=x, c_=c):
        w = z_ % 16
        return (y_ * 4 + w // 4, (x_ * 4 + w % 4) * 2 + c_)

    def remote(src, dst, send, recv, where):
        return pltpu.make_async_remote_copy(
            src_ref=src, dst_ref=dst, send_sem=send, recv_sem=recv, device_id=where, device_id_type=MESH
        )

    def drain(ref, sem):
        pltpu.make_async_copy(ref, ref, sem).wait()

    barrier = pltpu.get_barrier_semaphore()
    greet = [device(z + d) for d in (6, 10, 2, 14)]
    greet += [device(4 * g + 2 + (zs + d) % 4) for d in (1, 2, 3)]
    greet += [device(z, y_=y_up), device(z, y_=y_dn)]
    greet += [device(z, x_=(x + d) % 4) for d in (1, 2, 3)]
    greet += [device(z, c_=1 - c)]
    for where in greet:
        pl.semaphore_signal(barrier, inc=1, device_id=where, device_id_type=MESH)
    fetch = pltpu.make_async_copy(at_ref, an, fetched)
    fetch.start()
    fetch.wait()
    pk[:, :, 0:64] = an[:, 0:16, :]
    pk[:, :, 64:128] = an[:, 16:32, :]
    pl.semaphore_wait(barrier, len(greet))

    def lanes(s):
        return pl.ds(pl.multiple_of(s * CHUNK, CHUNK), CHUNK)

    def rows(start, size):
        return pl.ds(pl.multiple_of(start, 64), size)

    def send_b(s):
        for i in ORDER:
            h = (zh + i) % 4
            remote(
                bt_ref.at[h, :, lanes(s)], bt.at[s, rows(o * 64, 64)], b_send, b_recv.at[s], device(zl + 4 * h + 2)
            ).start()

    for i in ORDER:
        h = (zh + i) % 4
        remote(pk.at[h], ag.at[c, x, zl, zh], a_send.at[0], a_recv.at[0], device(zl + 4 * h + 2)).start()
    for s in range(AHEAD):
        send_b(s)

    own = rows(y * 256, 256)
    from_dn = rows(y_dn * 256, 256)
    from_up = rows(y_up * 256, 256)
    far = rows(((y + 2) % 4) * 256, 256)
    up_half = rows(y_dn * 256, 128)
    dn_half = rows(y_up * 256 + 128, 128)

    def step(s, carry):
        @pl.when(s < chunks)
        def _():
            drain(bt.at[s, own], b_recv.at[s])
            remote(bt.at[s, own], bt.at[s, own], up_send, up_recv.at[s], device(z, y_=y_up)).start()
            remote(bt.at[s, own], bt.at[s, own], dn_send, dn_recv.at[s], device(z, y_=y_dn)).start()

        @pl.when(s == 0)
        def _():
            drain(ag.at[c, x, zs], a_recv.at[0])
            for d in (1, 2, 3):
                there = device(4 * g + 2 + (zs + d) % 4)
                remote(ag.at[c, x, zs], ag.at[c, x, zs], a_send.at[1], a_recv.at[1], there).start()

        @pl.when(s + AHEAD < chunks)
        def _():
            send_b(s + AHEAD)

        @pl.when(jnp.logical_and(s >= 1, s < chunks + 1))
        def _():
            t = s - 1
            drain(bt.at[t, from_dn], up_recv.at[t])
            remote(bt.at[t, up_half], bt.at[t, up_half], ru_send, far_recv.at[t], device(z, y_=y_up)).start()
            drain(bt.at[t, from_up], dn_recv.at[t])
            remote(bt.at[t, dn_half], bt.at[t, dn_half], rd_send, far_recv.at[t], device(z, y_=y_dn)).start()

        @pl.when(s == 2)
        def _():
            drain(ag.at[c, x, pl.ds(0, 3)], a_recv.at[1])
            for d in (1, 2, 3):
                there = device(z, x_=(x + d) % 4)
                remote(ag.at[c, x], ag.at[c, x], a_send.at[2], a_recv.at[2], there).start()

        @pl.when(s == 3)
        def _():
            drain(ag.at[c, pl.ds(0, 3)], a_recv.at[2])
            remote(ag.at[c], ag.at[c], a_send.at[3], a_recv.at[3], device(z, c_=1 - c)).start()

        @pl.when(s == LAG)
        def _():
            drain(ag.at[1 - c], a_recv.at[3])

            def unpack(u, carry):
                low = lax.broadcasted_iota(jnp.int32, (16, 128), 1) < 64
                part = [ag[u % 2, u // 8, (u // 2) % 4, h] for h in range(4)]
                turned = [pltpu.roll(p, 64, 1) for p in part]
                for h in (0, 2):
                    side = pl.ds(64 * h, 128)
                    at[pl.ds(pl.multiple_of(u * 32, 16), 16), side] = jnp.where(low, part[h], turned[h + 1])
                    at[pl.ds(pl.multiple_of(u * 32 + 16, 16), 16), side] = jnp.where(low, turned[h], part[h + 1])
                return carry

            lax.fori_loop(0, 32, unpack, 0)

            def turn(k, carry):
                block = at[pl.ds(pl.multiple_of(k * 128, 128), 128), :].T
                high = block.astype(jnp.bfloat16)
                a_hi[:, pl.ds(pl.multiple_of(k * 128, 128), 128)] = high
                a_lo[:, pl.ds(pl.multiple_of(k * 128, 128), 128)] = (block - high.astype(jnp.float32)).astype(jnp.bfloat16)
                return carry

            lax.fori_loop(0, 8, turn, 0)

        @pl.when(s >= LAG)
        def _():
            t = s - LAG
            drain(bt.at[t, far], far_recv.at[t])
            block = bt[t]
            high = block.astype(jnp.bfloat16)
            low = (block - high.astype(jnp.float32)).astype(jnp.bfloat16)
            both = jnp.dot(a_hi[...], jnp.concatenate([high, low], axis=1), preferred_element_type=jnp.float32)
            cross = jnp.dot(a_lo[...], high, preferred_element_type=jnp.float32)
            cb[t] = 0.5 * (both[:, 0:CHUNK] + (both[:, CHUNK:] + cross))
            for i in ORDER:
                h = ((z + 2 + 4 * i) % 16) // 4
                remote(
                    cb.at[t, rows(64 * h, 64)], out_ref.at[g, :, lanes(t)], c_send, c_recv, device(4 * h + zs)
                ).start()

        return carry

    lax.fori_loop(0, chunks + LAG, step, 0)

    drain(out_ref, c_recv)
    drain(pk, a_send.at[0])
    drain(ag.at[c, x, pl.ds(0, 3)], a_send.at[1])
    drain(ag.at[c, pl.ds(0, 3)], a_send.at[2])
    drain(ag.at[c], a_send.at[3])
    drain(bt_ref, b_send)
    drain(cb, up_send)
    drain(cb, dn_send)
    drain(cb.at[:, pl.ds(0, 128)], ru_send)
    drain(cb.at[:, pl.ds(0, 128)], rd_send)
    drain(cb, c_send)


def body(amplitudes, integrals):
    at = pltpu.with_memory_space_constraint(jnp.swapaxes(amplitudes, 1, 2), pltpu.HBM)
    bt = pltpu.with_memory_space_constraint(jnp.swapaxes(integrals, 1, 2), pltpu.HBM)
    n_g, depth, cols = bt.shape
    chunks = cols // CHUNK
    f32, bf16 = jnp.float32, jnp.bfloat16
    dma = pltpu.SemaphoreType.DMA
    return pl.pallas_call(
        kernel,
        out_shape=jax.ShapeDtypeStruct((n_g, 64, cols), f32),
        in_specs=[pl.BlockSpec(memory_space=pl.ANY), pl.BlockSpec(memory_space=pl.ANY)],
        out_specs=pl.BlockSpec(memory_space=pl.ANY),
        scratch_shapes=[
            pltpu.VMEM((4, 32, 64), f32),
            pltpu.VMEM((4, 16, 128), f32),
            pltpu.VMEM((2, 4, 4, 4, 16, 128), f32),
            pltpu.VMEM((1024, 256), f32),
            pltpu.VMEM((256, 1024), bf16),
            pltpu.VMEM((256, 1024), bf16),
            pltpu.VMEM((chunks, 1024, CHUNK), f32),
            pltpu.VMEM((chunks, 256, CHUNK), f32),
            dma((4,)),
            dma((4,)),
            dma,
            dma((chunks,)),
            dma,
            dma((chunks,)),
            dma,
            dma((chunks,)),
            dma,
            dma,
            dma((chunks,)),
            dma,
            dma,
            dma,
        ],
        compiler_params=pltpu.CompilerParams(collective_id=0, has_side_effects=True, vmem_limit_bytes=20 * 2**20),
    )(at, bt)


def solution(mesh):
    in_specs = (P(None, "occ", "vir"), P(None, "vir", "occ"))
    out_specs = P(None, "occ", "vir")
    return jax.shard_map(body, mesh=mesh, in_specs=in_specs, out_specs=out_specs, check_vma=False)
```
